256 devices in a mesh: form: 16 (over x_hi, y, core), cond: 16 (over x_lo, z).
Axes of the slice: x: 4 (x_hi: 2, x_lo: 2; x = x_hi * 2 + x_lo), y: 4, z: 8, core: 2. Of those that a mesh axis runs over, the one named last changes fastest.
Arguments:
- field: float32 [131072, 2048], P('form', 'cond'), may hold values from -6 to 6
- kf_blocks: float32 [1024, 5, 128, 128], P(('form', 'cond')), may hold values from -0.375 to 0.375
- kf_cols: int32 [1024, 5], P(('form', 'cond')), may hold values from 0 to 1023, as said below
- kf_counts: int32 [1024], P(('form', 'cond')), may hold values from 1 to 5, as said below
- kc_blocks: float32 [16, 4, 128, 128], P('cond'), may hold values from -0.375 to 0.375
- kc_cols: int32 [16, 4], replicated, may hold values from 0 to 15, as said below
- kc_counts: int32 [16], replicated, may hold values from 1 to 4, as said below
Outputs:
- product: float32 [131072, 2048], P('form', 'cond')
The draws below stay inside these ranges and needn't reach their ends.
Inputs may be any that keep to these rules, and one draw needn't show every extreme that they name: kf_cols[r, s] lies within 2 of r; slot 0 is r itself, the live slots (s < kf_counts[r]) of a row are distinct, the others repeat r. `kf_counts`: some block rows in every draw have all 5 slots live. `kc_cols`: slot 0 is r itself, the live slots (s < kc_counts[r]) of a row are distinct, the others repeat r. `kc_counts`: block row 0 has all 4 slots live.
All inputs are finite; a program needn't handle non-finite values.
Results may differ from the reference program's by a relative error of at most 0.0003.
Values sent between devices are 32-bit elements; how exact they have to be, the bound alone decides.
No kernel may reach another device: no remote copies, remote signals or barrier semaphores. Data moves between devices by JAX's collectives and lax.ppermute only.
A program may use at most 128 MiB of HBM per device.

```python
import jax
import jax.numpy as jnp
from jax import lax

BLK = 128
HB = 2
NNZ_F = 5
NNZ_C = 4
NF = 131072
NCB = 16
NC = 2048
NBF = 1024


def formulation_pattern(key):
    level = jax.random.randint(jax.random.fold_in(key, 11), (NBF,), 0, 4)
    coins = jax.random.randint(jax.random.fold_in(key, 12), (NBF, NNZ_F), 0, 4)
    rows = jnp.arange(NBF, dtype=jnp.int32)
    slots = jnp.arange(NNZ_F, dtype=jnp.int32)
    offsets = jnp.where(slots % 2 == 1, -((slots + 1) // 2), slots // 2)
    cols = rows[:, None] + offsets[None, :]
    keep = (coins < level[:, None]) | (rows % 7 == 3)[:, None] | (slots == 0)[None, :]
    keep = keep & (cols >= 0) & (cols < NBF)
    score = jnp.where(keep, slots[None, :], slots[None, :] + NNZ_F)
    order = jnp.argsort(score, axis=1)
    kept_sorted = jnp.take_along_axis(keep, order, axis=1)
    cols_sorted = jnp.take_along_axis(cols, order, axis=1)
    final = jnp.where(kept_sorted, cols_sorted, rows[:, None])
    return (final.astype(jnp.int32), jnp.sum(keep.astype(jnp.int32), axis=1).astype(jnp.int32))


def condition_pattern(key):
    keys = jax.random.split(jax.random.fold_in(key, 21), NCB)
    perms = jax.vmap(lambda single: jax.random.permutation(single, NCB))(keys).astype(jnp.int32)
    rows = jnp.arange(NCB, dtype=jnp.int32)
    is_self = (perms == rows[:, None]).astype(jnp.int32)
    order = jnp.argsort(is_self, axis=1, stable=True)
    others = jnp.take_along_axis(perms, order, axis=1)[:, :NNZ_C - 1]
    cols = jnp.concatenate([rows[:, None], others], axis=1)
    count = jax.random.randint(jax.random.fold_in(key, 22), (NCB,), 1, NNZ_C + 1)
    count = jnp.where(rows == 0, NNZ_C, count).astype(jnp.int32)
    slots = jnp.arange(NNZ_C, dtype=jnp.int32)
    cols = jnp.where(slots[None, :] < count[:, None], cols, rows[:, None])
    return (cols.astype(jnp.int32), count)


def draw_kf_cols(key, part):
    return formulation_pattern(key)[0]


def draw_kf_counts(key, part):
    return formulation_pattern(key)[1]


def draw_kc_cols(key, part):
    return condition_pattern(key)[0]


def draw_kc_counts(key, part):
    return condition_pattern(key)[1]


def shard_levels(stream_key, dims, shards, low, high):
    loudness = 1.0
    for dim, shards_of in shards:
        steps = jax.random.uniform(jax.random.fold_in(jax.random.fold_in(stream_key, 6), dim), (shards_of,), jnp.float32, low / len(shards), high / len(shards))
        loudness = loudness * jnp.repeat(jnp.exp(steps), dims[dim] // shards_of).reshape((-1,) + (1,) * (len(dims) - 1 - dim))
    return loudness


def scatter_about(rng, dims, scale, limit, cuts=(), kind=jnp.bfloat16):
    array = jax.random.normal(rng, dims, jnp.float32) * scale
    if len(cuts) > 0:
        array = shard_levels(rng, dims, cuts, -0.22, 0.18) * array
    return jnp.clip(array, min=-limit, max=limit).astype(kind)


def setup_inputs(seed: int = 0) -> dict:
    key_of = jax.random.split(jax.random.key(seed), 8)
    field = scatter_about(key_of[0], (NF, NC), 1.0, 6.0, ((0, 16), (1, 16)), jnp.float32)
    kf_blocks = scatter_about(key_of[1], (NBF, NNZ_F, BLK, BLK), (BLK * HB) ** -0.5, 0.375, ((0, 256),), jnp.float32)
    kf_cols = draw_kf_cols(jax.random.fold_in(key_of[7], 71), 0)
    kf_counts = draw_kf_counts(jax.random.fold_in(key_of[7], 71), 0)
    kc_blocks = scatter_about(key_of[4], (NCB, NNZ_C, BLK, BLK), (BLK * 2) ** -0.5, 0.375, ((0, 16),), jnp.float32)
    kc_cols = draw_kc_cols(jax.random.fold_in(key_of[7], 71), 0)
    kc_counts = draw_kc_counts(jax.random.fold_in(key_of[7], 71), 0)
    return dict(field=field, kf_blocks=kf_blocks, kf_cols=kf_cols, kf_counts=kf_counts, kc_blocks=kc_blocks, kc_cols=kc_cols, kc_counts=kc_counts)


def reference(field, kf_blocks, kf_cols, kf_counts, kc_blocks, kc_cols, kc_counts):
    hi = lax.Precision.HIGHEST
    field_blocks = field.reshape(NBF, BLK, NC)

    def formulation_row(items):
        blocks, cols, count = items
        total = jnp.zeros((BLK, NC), jnp.float32)
        for slot in range(NNZ_F):
            term = jnp.dot(blocks[slot], field_blocks[cols[slot]], precision=hi)
            total = total + jnp.where(slot < count, term, 0.0)
        return total

    inner = lax.map(formulation_row, (kf_blocks, kf_cols, kf_counts))
    targets = jnp.arange(NCB, dtype=jnp.int32)
    routes = []
    for slot in range(NNZ_C):
        live = (kc_cols[:, slot][:, None] == targets[None, :]) & (slot < kc_counts)[:, None]
        routes.append(live.astype(jnp.float32))

    def condition_row(block):
        parts = block.reshape(BLK, NCB, BLK)
        total = jnp.zeros((BLK, NCB, BLK), jnp.float32)
        for slot in range(NNZ_C):
            moved = jnp.einsum("prc,rcd->prd", parts, kc_blocks[:, slot], precision=hi)
            total = total + jnp.einsum("prd,rk->pkd", moved, routes[slot], precision=hi)
        return total.reshape(BLK, NC)

    product = lax.map(condition_row, inner)
    return product.reshape(NF, NC)
```

```python
import jax
import jax.numpy as jnp
from jax import lax
from jax.experimental import pallas as pl
from jax.experimental.pallas import tpu as pltpu
from jax.sharding import PartitionSpec as P

NX = 2
BF = jnp.bfloat16
F32 = jnp.float32
SMEM = pl.BlockSpec(memory_space=pltpu.SMEM)


MIB = 1 << 20


def params(mib):
    return pltpu.CompilerParams(vmem_limit_bytes=mib * MIB)


def cost(flops, byte):
    return pl.CostEstimate(flops=flops, transcendentals=0, bytes_accessed=byte)


def split(value):
    high = value.astype(BF)
    return high, (value - high.astype(F32)).astype(BF)


def dot(a, b):
    return jnp.dot(a, b, preferred_element_type=F32)


def form_kernel_build(scalars, cols, counts, blocks, mid, low, high, dense):
    rows, slots, blk, _ = blocks.shape
    reach = (slots - 1) // 2
    dense[...] = jnp.zeros_like(dense)
    for k in range(rows):
        for s in range(slots):
            place = cols[k, s] - scalars[0] + reach

            @pl.when(s < counts[k])
            def _():
                dense[place, pl.ds(k * blk, blk), :] = blocks[k, s]

    size = rows * blk
    half = reach * blk
    for j in range(rows):
        a, b = split(dense[reach + j])
        mid[pl.ds(0, size), pl.ds(j * blk, blk)] = a
        mid[pl.ds(size, size), pl.ds(j * blk, blk)] = b
    for j in range(reach):
        a, b = split(dense[j, pl.ds(0, half), :])
        low[pl.ds(0, half), pl.ds(j * blk, blk)] = a
        low[pl.ds(half, half), pl.ds(j * blk, blk)] = b
        a, b = split(dense[reach + rows + j, pl.ds(size - half, half), :])
        high[pl.ds(0, half), pl.ds(j * blk, blk)] = a
        high[pl.ds(half, half), pl.ds(j * blk, blk)] = b


def cond_kernel_build(nz, scalars, cols, counts, pieces, upper, lower):
    nf, nb, part, blk = pieces.shape
    slots = cols.shape[1]
    per = blk // part
    step = pl.program_id(0)
    f, c = scalars[1], scalars[2]
    x, z = c // nz, c % nz
    upper[...] = jnp.zeros_like(upper)
    lower[...] = jnp.zeros_like(lower)

    def source(q, carry):
        for slot in range(slots):
            d = cols[q, slot]
            tdx = (d // nz) ^ x
            tdz = ((d % nz) - z) & (nz - 1)

            @pl.when((slot < counts[q]) & (tdz == step))
            def _():
                for i in range(per):
                    a, b = split(pieces[f ^ (slot * per + i), c ^ q])
                    at = pl.ds(pl.multiple_of(q * blk + i * part, part), part)
                    upper[tdx, at, :] = a
                    lower[tdx, at, :] = b

        return carry

    lax.fori_loop(0, nb, source, 0)


def place_rows(count, scalars, *refs):
    blocks, out, sems = refs[:count], refs[-2], refs[-1]
    size = blocks[0].shape[0]
    copies = [
        pltpu.make_async_copy(block, out.at[pl.ds(scalars[i] * size, size), :], sems.at[i])
        for i, block in enumerate(blocks)
    ]
    for copy in copies:
        copy.start()
    for copy in copies:
        copy.wait()


def form_product(kmid, klow, khigh, field, low, high, out):
    def beside(ref):
        return jnp.concatenate([ref[i] for i in range(NX)], axis=1)

    size = field.shape[1]
    half = low.shape[1]

    def three(k, v):
        n = k.shape[0] // 2
        a, b = split(v)
        both = dot(k[...], a)
        return both[:n] + both[n:] + dot(k[pl.ds(0, n), :], b)

    total = three(kmid, beside(field))
    top = total[:half] + three(klow, beside(low))
    bottom = total[size - half:] + three(khigh, beside(high))
    inside = [total[half:size - half]] if size > 2 * half else []
    a, b = split(jnp.concatenate([top] + inside + [bottom], axis=0))
    out[pl.ds(0, size), :] = a
    out[pl.ds(size, size), :] = b


def cond_product(nz, *refs):
    inner, (upper, lower), outs = refs[:nz], refs[nz:nz + 2], refs[nz + 2:]
    size = inner[0].shape[0] // 2
    blk = upper.shape[2]
    both = jnp.zeros((2 * size, NX * blk), F32)
    cross = jnp.zeros((size, NX * blk), F32)
    for p in range(nz):
        at = pl.ds(p * NX * blk, NX * blk)
        u = jnp.concatenate([upper[i, at, :] for i in range(NX)], axis=1)
        w = jnp.concatenate([lower[i, at, :] for i in range(NX)], axis=1)
        both = both + dot(inner[p][...], u)
        cross = cross + dot(inner[p][pl.ds(0, size), :], w)
    result = both[:size] + both[size:] + cross
    for i in range(NX):
        outs[i][...] = result[:, i * blk:(i + 1) * blk]


def body(field, kf_blocks, kf_cols, kf_counts, kc_blocks, kc_cols, kc_counts):
    rows_dev, slot_count, blk, _ = kf_blocks.shape
    reach = (slot_count - 1) // 2
    size = rows_dev * blk
    edge = reach * blk
    nf, nc = lax.axis_size("form"), lax.axis_size("cond")
    nz = nc // NX
    f, c = lax.axis_index("form"), lax.axis_index("cond")
    x, z = c // nz, c % nz
    first_row = (f * nc + c) * rows_dev
    scalars = jnp.stack([first_row, f, c, (z == 0).astype(jnp.int32), (z == nz - 1).astype(jnp.int32)]).astype(jnp.int32)

    def move(value, dx, dz):
        pairs = [
            (a * nz + b, (a ^ dx) * nz + (b + dz) % nz) for a in range(NX) for b in range(nz)
        ]
        return lax.ppermute(value, "cond", pairs)

    def gate(value, *earlier):
        return lax.optimization_barrier((value,) + earlier)[0]

    part = kc_blocks.shape[1] * blk // nf
    pieces = lax.dynamic_slice_in_dim(kc_blocks.reshape(-1, blk), f * part, part, axis=0)[None]

    def spread(value, axis, count, low, bits):
        got = [value] + [
            lax.ppermute(value, axis, [(i, i ^ (e << low)) for i in range(count)]) for e in range(1, 1 << bits)
        ]
        return jnp.stack(got, axis=1).reshape((-1,) + value.shape[1:])

    pieces = spread(pieces, "cond", nc, 2, 2)
    pieces = spread(pieces, "cond", nc, 0, 2)[None]

    field, pieces = lax.optimization_barrier((field, pieces))
    regrouped = lax.all_to_all(field.reshape(nc, size, blk), "cond", 0, 0, tiled=True)

    pieces = spread(pieces, "form", nf, 3, 1)
    pieces = spread(pieces, "form", nf, 1, 2)
    pieces = spread(pieces, "form", nf, 0, 1)

    band = rows_dev + 2 * reach
    kmid, klow, khigh = pl.pallas_call(
        form_kernel_build,
        out_shape=(
            jax.ShapeDtypeStruct((2 * size, size), BF),
            jax.ShapeDtypeStruct((2 * edge, edge), BF),
            jax.ShapeDtypeStruct((2 * edge, edge), BF),
        ),
        in_specs=[SMEM, SMEM, SMEM, pl.BlockSpec(memory_space=pltpu.VMEM)],
        scratch_shapes=[pltpu.VMEM((band, size, blk), F32)],
        compiler_params=params(8),
        cost_estimate=cost(0, 8 * MIB),
        name="form_kernel_build",
    )(scalars, kf_cols, kf_counts, kf_blocks)

    width = nc * blk
    upper, lower = pl.pallas_call(
        lambda *refs: cond_kernel_build(nz, *refs),
        grid=(nz,),
        out_shape=(pltpu.HBM((nc, width, blk), BF),) * 2,
        in_specs=[SMEM, SMEM, SMEM, pl.BlockSpec(pieces.shape, lambda t: (0, 0, 0, 0))],
        out_specs=(pl.BlockSpec((NX, width, blk), lambda t: (t, 0, 0)),) * 2,
        compiler_params=params(16),
        cost_estimate=cost(0, 32 * MIB),
        name="cond_kernel_build",
    )(scalars, kc_cols, kc_counts, pieces)

    total = nf * nc
    regrouped = gate(regrouped, upper, kmid)
    per = 4
    inner = []

    def whole(a):
        return pl.BlockSpec(a.shape, lambda i: (0,) * a.ndim)

    for start in range(0, nc, per):
        columns = lax.slice_in_dim(regrouped, start, start + per, axis=0)
        from_low = lax.ppermute(columns[:, size - edge:], ("form", "cond"), [(i, i + 1) for i in range(total - 1)])
        from_high = lax.ppermute(columns[:, :edge], ("form", "cond"), [(i + 1, i) for i in range(total - 1)])
        for at in range(0, per, NX):
            args = (kmid, klow, khigh)
            place = (start + at) // NX
            inner.append(pl.pallas_call(
                form_product,
                grid=(1,),
                out_shape=jax.ShapeDtypeStruct((2 * size, NX * blk), BF),
                in_specs=[whole(a) for a in args] + [
                    pl.BlockSpec((NX, size, blk), lambda i, place=place: (place, 0, 0)),
                    pl.BlockSpec((NX, edge, blk), lambda i, at=at: (at // NX, 0, 0)),
                    pl.BlockSpec((NX, edge, blk), lambda i, at=at: (at // NX, 0, 0)),
                ],
                out_specs=pl.BlockSpec((2 * size, NX * blk), lambda i: (0, 0)),
                compiler_params=params(8),
                cost_estimate=cost(0, 8 * MIB),
                name="form_product",
            )(*args, regrouped, from_low, from_high))

    received = []
    for dz in (4, 3, 5, 2, 6, 1, 7, 0):
        spec = pl.BlockSpec((NX, width, blk), lambda i, dz=dz: (dz, 0, 0))
        results = pl.pallas_call(
            lambda *refs: cond_product(nz, *refs),
            grid=(1,),
            out_shape=(jax.ShapeDtypeStruct((size, blk), F32),) * NX,
            in_specs=[whole(a) for a in inner] + [spec, spec],
            out_specs=(pl.BlockSpec((size, blk), lambda i: (0, 0)),) * NX,
            compiler_params=params(14),
            cost_estimate=cost(0, 14 * MIB),
            name="cond_product",
        )(*inner, upper, lower)
        for dx in reversed(range(NX)):
            got = results[dx] if dz == 0 and dx == 0 else move(results[dx], dx, dz)
            received.append(((x ^ dx) * nz + (z - dz) % nz, got))

    out = None
    for batch in (received[:10], received[10:]):
        count = len(batch)
        places = jnp.stack([place for place, _ in batch]).astype(jnp.int32)
        blocks = [block for _, block in batch] + ([] if out is None else [out])
        out = pl.pallas_call(
            lambda *refs, count=count: place_rows(count, *refs),
            out_shape=jax.ShapeDtypeStruct((nc * size, blk), F32),
            in_specs=[SMEM] + [pl.BlockSpec(memory_space=pltpu.VMEM)] * count + [pl.BlockSpec(memory_space=pltpu.HBM)] * (len(blocks) - count),
            out_specs=pl.BlockSpec(memory_space=pltpu.HBM),
            scratch_shapes=[pltpu.SemaphoreType.DMA((count,))],
            input_output_aliases={} if out is None else {len(blocks): 0},
            compiler_params=params(6),
            cost_estimate=cost(0, 4 * MIB),
            name="place_rows",
        )(places, *blocks)
    return out


def solution(mesh):
    in_specs = (
        P("form", "cond"),
        P(("form", "cond"), None, None, None),
        P(("form", "cond"), None),
        P(("form", "cond")),
        P("cond", None, None, None),
        P(),
        P(),
    )
    out_specs = P("form", "cond")
    return jax.shard_map(body, mesh=mesh, in_specs=in_specs, out_specs=out_specs, check_vma=False)
```

```python
import jax
import jax.numpy as jnp
from jax import lax
from jax.experimental import pallas as pl
from jax.experimental.pallas import tpu as pltpu
from jax.sharding import PartitionSpec as P

NX = 2
BF = jnp.bfloat16
F32 = jnp.float32
SMEM = pl.BlockSpec(memory_space=pltpu.SMEM)


MIB = 1 << 20


def params(mib):
    return pltpu.CompilerParams(vmem_limit_bytes=mib * MIB)


def cost(flops, byte):
    return pl.CostEstimate(flops=flops, transcendentals=0, bytes_accessed=byte)


def split(value):
    high = value.astype(BF)
    return high, (value - high.astype(F32)).astype(BF)


def dot(a, b):
    return jnp.dot(a, b, preferred_element_type=F32)


def form_kernel_build(scalars, cols, counts, blocks, mid, low, high, dense):
    rows, slots, blk, _ = blocks.shape
    reach = (slots - 1) // 2
    dense[...] = jnp.zeros_like(dense)
    for k in range(rows):
        for s in range(slots):
            place = cols[k, s] - scalars[0] + reach

            @pl.when(s < counts[k])
            def _():
                dense[place, pl.ds(k * blk, blk), :] = blocks[k, s]

    size = rows * blk
    half = reach * blk
    for j in range(rows):
        a, b = split(dense[reach + j])
        mid[pl.ds(0, size), pl.ds(j * blk, blk)] = a
        mid[pl.ds(size, size), pl.ds(j * blk, blk)] = b
    for j in range(reach):
        a, b = split(dense[j, pl.ds(0, half), :])
        low[pl.ds(0, half), pl.ds(j * blk, blk)] = a
        low[pl.ds(half, half), pl.ds(j * blk, blk)] = b
        a, b = split(dense[reach + rows + j, pl.ds(size - half, half), :])
        high[pl.ds(0, half), pl.ds(j * blk, blk)] = a
        high[pl.ds(half, half), pl.ds(j * blk, blk)] = b


def cond_kernel_build(nz, scalars, cols, counts, pieces, upper, lower):
    nf, nb, part, blk = pieces.shape
    slots = cols.shape[1]
    per = blk // part
    step = pl.program_id(0)
    f, c = scalars[1], scalars[2]
    bits = nz.bit_length() - 1
    x, wanted = c >> bits, (c + scalars[5 + step]) & (nz - 1)
    upper[...] = jnp.zeros_like(upper)
    lower[...] = jnp.zeros_like(lower)

    def source(q, carry):
        for slot in range(slots):
            d = cols[q, slot]
            tdx = (d >> bits) ^ x

            @pl.when((slot < counts[q]) & ((d & (nz - 1)) == wanted))
            def _():
                for i in range(per):
                    a, b = split(pieces[f ^ (slot * per + i), q])
                    at = pl.ds(pl.multiple_of(q * blk + i * part, part), part)
                    upper[tdx, at, :] = a
                    lower[tdx, at, :] = b

        return carry

    lax.fori_loop(0, nb, source, 0)


def place_rows(count, scalars, *refs):
    blocks, out, sems = refs[:count], refs[-2], refs[-1]
    size = blocks[0].shape[0]
    copies = [
        pltpu.make_async_copy(block, out.at[pl.ds(scalars[i] * size, size), :], sems.at[i])
        for i, block in enumerate(blocks)
    ]
    for copy in copies:
        copy.start()
    for copy in copies:
        copy.wait()


def form_product(kmid, klow, khigh, field, low, high, out):
    def beside(ref):
        return jnp.concatenate([ref[i] for i in range(NX)], axis=1)

    size = field.shape[1]
    half = low.shape[1]

    def three(k, v):
        n = k.shape[0] // 2
        a, b = split(v)
        both = dot(k[...], a)
        return both[:n] + both[n:] + dot(k[pl.ds(0, n), :], b)

    total = three(kmid, beside(field))
    top = total[:half] + three(klow, beside(low))
    bottom = total[size - half:] + three(khigh, beside(high))
    inside = [total[half:size - half]] if size > 2 * half else []
    a, b = split(jnp.concatenate([top] + inside + [bottom], axis=0))
    out[0, pl.ds(0, size), :] = a
    out[0, pl.ds(size, size), :] = b


def cond_product(count, *refs):
    inner, (upper, lower), outs = refs[:count], refs[count:count + 2], refs[count + 2:]
    size = inner[0].shape[1] // 2
    blk = upper.shape[2]
    both = jnp.zeros((2 * size, NX * blk), F32)
    cross = jnp.zeros((size, NX * blk), F32)
    parts = [(ref, i) for ref in inner for i in range(ref.shape[0])]
    for p, (ref, i) in enumerate(parts):
        at = pl.ds(p * NX * blk, NX * blk)
        u = jnp.concatenate([upper[i, at, :] for i in range(NX)], axis=1)
        w = jnp.concatenate([lower[i, at, :] for i in range(NX)], axis=1)
        both = both + dot(ref[i], u)
        cross = cross + dot(ref[i, pl.ds(0, size), :], w)
    result = both[:size] + both[size:] + cross
    for t in range(len(outs) // NX):

        @pl.when(pl.program_id(0) == t)
        def _():
            for i in range(NX):
                outs[t * NX + i][...] = result[:, i * blk:(i + 1) * blk]


def body(field, kf_blocks, kf_cols, kf_counts, kc_blocks, kc_cols, kc_counts):
    rows_dev, slot_count, blk, _ = kf_blocks.shape
    reach = (slot_count - 1) // 2
    size = rows_dev * blk
    edge = reach * blk
    nf, nc = lax.axis_size("form"), lax.axis_size("cond")
    nz = nc // NX
    f, c = lax.axis_index("form"), lax.axis_index("cond")
    x, z = c // nz, c % nz
    first_row = (f * nc + c) * rows_dev
    order = (4, 3, 5, 2, 6, 1, 7, 0)
    scalars = jnp.stack([first_row, f, c, c, c] + list(order)).astype(jnp.int32)

    def move(value, dx, dz):
        pairs = [
            (a * nz + b, (a ^ dx) * nz + (b + dz) % nz) for a in range(NX) for b in range(nz)
        ]
        return lax.ppermute(value, "cond", pairs)

    def gate(value, *earlier):
        return lax.optimization_barrier((value,) + earlier)[0]

    part = kc_blocks.shape[1] * blk // nf
    piece = lax.dynamic_slice_in_dim(kc_blocks.reshape(-1, blk), f * part, part, axis=0)
    total = nf * nc

    def crossed(value, flip):
        return lax.ppermute(value, ("form", "cond"), [(i, i ^ flip) for i in range(total)])

    pieces = lax.all_to_all(jnp.broadcast_to(piece[None], (nc, part, blk)), "cond", 0, 0, tiled=True)
    field = gate(field, pieces)
    regrouped = lax.all_to_all(field.reshape(nc, size, blk), "cond", 0, 0, tiled=True)

    pieces = jnp.stack([pieces, crossed(pieces, total // 2)]).reshape((NX, 1, nc, part, blk))
    pieces = jnp.concatenate([pieces] + [crossed(pieces, i * 2 * nc) for i in range(1, nf // 4)], axis=1)
    pieces = jnp.stack([pieces, crossed(pieces, nc)], axis=2).reshape((nf, nc, part, blk))

    band = rows_dev + 2 * reach
    kmid, klow, khigh = pl.pallas_call(
        form_kernel_build,
        out_shape=(
            jax.ShapeDtypeStruct((2 * size, size), BF),
            jax.ShapeDtypeStruct((2 * edge, edge), BF),
            jax.ShapeDtypeStruct((2 * edge, edge), BF),
        ),
        in_specs=[SMEM, SMEM, SMEM, pl.BlockSpec(memory_space=pltpu.VMEM)],
        scratch_shapes=[pltpu.VMEM((band, size, blk), F32)],
        compiler_params=params(8),
        cost_estimate=cost(0, 8 * MIB),
        name="form_kernel_build",
    )(scalars, kf_cols, kf_counts, kf_blocks)

    width = nc * blk
    upper, lower = pl.pallas_call(
        lambda *refs: cond_kernel_build(nz, *refs),
        grid=(nz,),
        out_shape=(pltpu.HBM((nc, width, blk), BF),) * 2,
        in_specs=[SMEM, SMEM, SMEM, pl.BlockSpec(pieces.shape, lambda t: (0, 0, 0, 0))],
        out_specs=(pl.BlockSpec((NX, width, blk), lambda t: (t, 0, 0)),) * 2,
        compiler_params=params(16),
        cost_estimate=cost(0, 32 * MIB),
        name="cond_kernel_build",
    )(scalars, kc_cols, kc_counts, pieces)

    regrouped = gate(regrouped, upper, kmid)
    inner = []

    def whole(a):
        return pl.BlockSpec(a.shape, lambda i: (0,) * a.ndim)

    start = 0
    for per in (4, 4, 4, 4):
        columns = lax.slice_in_dim(lax.optimization_barrier(regrouped), start, start + per, axis=0)
        from_low = lax.ppermute(columns[:, size - edge:], ("form", "cond"), [(i, i + 1) for i in range(total - 1)])
        from_high = lax.ppermute(columns[:, :edge], ("form", "cond"), [(i + 1, i) for i in range(total - 1)])
        args = (kmid, klow, khigh)
        place = start // NX
        inner.append(pl.pallas_call(
            form_product,
            grid=(per // NX,),
            out_shape=jax.ShapeDtypeStruct((per // NX, 2 * size, NX * blk), BF),
            in_specs=[whole(a) for a in args] + [
                pl.BlockSpec((NX, size, blk), lambda i, place=place: (place + i, 0, 0)),
                pl.BlockSpec((NX, edge, blk), lambda i: (i, 0, 0)),
                pl.BlockSpec((NX, edge, blk), lambda i: (i, 0, 0)),
            ],
            out_specs=pl.BlockSpec((1, 2 * size, NX * blk), lambda i: (i, 0, 0)),
            compiler_params=params(12),
            cost_estimate=cost(0, 8 * MIB),
            name="form_product",
        )(*args, regrouped, from_low, from_high))
        start += per

    received = []
    for done, count in ((3, 5), (1, 2), (0, 1)):
        spec = pl.BlockSpec((NX, width, blk), lambda i, done=done: (done + i, 0, 0))
        results = pl.pallas_call(
            lambda *refs: cond_product(len(inner), *refs),
            grid=(count,),
            out_shape=(jax.ShapeDtypeStruct((size, blk), F32),) * (NX * count),
            in_specs=[whole(a) for a in inner] + [spec, spec],
            out_specs=(pl.BlockSpec((size, blk), lambda i: (0, 0)),) * (NX * count),
            compiler_params=params(20),
            cost_estimate=cost(0, 14 * MIB * count),
            name="cond_product",
        )(*inner, upper, lower)
        for i, dz in reversed(list(enumerate(order[done:done + count]))):
            for dx in reversed(range(NX)):
                one = results[i * NX + dx]
                got = one if dz == 0 and dx == 0 else move(one, dx, dz)
                received.append(((x ^ dx) * nz + (z - dz) % nz, got))
    out = None
    for batch in (received[-10:], received[:-10]):
        count = len(batch)
        places = jnp.stack([place for place, _ in batch]).astype(jnp.int32)
        blocks = [block for _, block in batch] + ([] if out is None else [out])
        out = pl.pallas_call(
            lambda *refs, count=count: place_rows(count, *refs),
            out_shape=jax.ShapeDtypeStruct((nc * size, blk), F32),
            in_specs=[SMEM] + [pl.BlockSpec(memory_space=pltpu.VMEM)] * count + [pl.BlockSpec(memory_space=pltpu.HBM)] * (len(blocks) - count),
            out_specs=pl.BlockSpec(memory_space=pltpu.HBM),
            scratch_shapes=[pltpu.SemaphoreType.DMA((count,))],
            input_output_aliases={} if out is None else {len(blocks): 0},
            compiler_params=params(6),
            cost_estimate=cost(0, 4 * MIB),
            name="place_rows",
        )(places, *blocks)
    return out


def solution(mesh):
    in_specs = (
        P("form", "cond"),
        P(("form", "cond"), None, None, None),
        P(("form", "cond"), None),
        P(("form", "cond")),
        P("cond", None, None, None),
        P(),
        P(),
    )
    out_specs = P("form", "cond")
    return jax.shard_map(body, mesh=mesh, in_specs=in_specs, out_specs=out_specs, check_vma=False)
```

```python
import jax
import jax.numpy as jnp
from jax import lax
from jax.experimental import pallas as pl
from jax.experimental.pallas import tpu as pltpu
from jax.sharding import PartitionSpec as P

NX = 2
BF = jnp.bfloat16
F32 = jnp.float32
SMEM = pl.BlockSpec(memory_space=pltpu.SMEM)


MIB = 1 << 20


def params(mib):
    return pltpu.CompilerParams(vmem_limit_bytes=mib * MIB)


def cost(flops, byte):
    return pl.CostEstimate(flops=flops, transcendentals=0, bytes_accessed=byte)


def split(value):
    high = value.astype(BF)
    return high, (value - high.astype(F32)).astype(BF)


def dot(a, b):
    return jnp.dot(a, b, preferred_element_type=F32)


def form_kernel_build(scalars, cols, counts, blocks, mid, low, high, dense):
    rows, slots, blk, _ = blocks.shape
    reach = (slots - 1) // 2
    dense[...] = jnp.zeros_like(dense)
    for k in range(rows):
        for s in range(slots):
            place = cols[k, s] - scalars[0] + reach

            @pl.when(s < counts[k])
            def _():
                dense[place, pl.ds(k * blk, blk), :] = blocks[k, s]

    size = rows * blk
    half = reach * blk
    for j in range(rows):
        a, b = split(dense[reach + j])
        mid[pl.ds(0, size), pl.ds(j * blk, blk)] = a
        mid[pl.ds(size, size), pl.ds(j * blk, blk)] = b
    for j in range(reach):
        a, b = split(dense[j, pl.ds(0, half), :])
        low[pl.ds(0, half), pl.ds(j * blk, blk)] = a
        low[pl.ds(half, half), pl.ds(j * blk, blk)] = b
        a, b = split(dense[reach + rows + j, pl.ds(size - half, half), :])
        high[pl.ds(0, half), pl.ds(j * blk, blk)] = a
        high[pl.ds(half, half), pl.ds(j * blk, blk)] = b


def cond_kernel_build(nz, scalars, cols, counts, pieces, upper, lower):
    nf, nb, part, blk = pieces.shape
    slots = cols.shape[1]
    per = blk // part
    step = pl.program_id(0)
    f, c = scalars[1], scalars[2]
    bits = nz.bit_length() - 1
    x, wanted = c >> bits, (c + scalars[5 + step]) & (nz - 1)
    upper[...] = jnp.zeros_like(upper)
    lower[...] = jnp.zeros_like(lower)

    def source(q, carry):
        for slot in range(slots):
            d = cols[q, slot]
            tdx = (d >> bits) ^ x

            @pl.when((slot < counts[q]) & ((d & (nz - 1)) == wanted))
            def _():
                for i in range(per):
                    a, b = split(pieces[f ^ (slot * per + i), q ^ (x << bits)])
                    at = pl.ds(pl.multiple_of(q * blk + i * part, part), part)
                    upper[tdx, at, :] = a
                    lower[tdx, at, :] = b

        return carry

    lax.fori_loop(0, nb, source, 0)


def place_rows(count, scalars, *refs):
    blocks, out, sems = refs[:count], refs[-2], refs[-1]
    size = blocks[0].shape[0]
    copies = [
        pltpu.make_async_copy(block, out.at[pl.ds(scalars[i] * size, size), :], sems.at[i])
        for i, block in enumerate(blocks)
    ]
    for copy in copies:
        copy.start()
    for copy in copies:
        copy.wait()


def form_product(kmid, klow, khigh, field, low, high, out):
    def beside(ref):
        return jnp.concatenate([ref[i] for i in range(NX)], axis=1)

    size = field.shape[1]
    half = low.shape[1]

    def three(k, v):
        n = k.shape[0] // 2
        a, b = split(v)
        both = dot(k[...], a)
        return both[:n] + both[n:] + dot(k[pl.ds(0, n), :], b)

    total = three(kmid, beside(field))
    top = total[:half] + three(klow, beside(low))
    bottom = total[size - half:] + three(khigh, beside(high))
    inside = [total[half:size - half]] if size > 2 * half else []
    a, b = split(jnp.concatenate([top] + inside + [bottom], axis=0))
    out[0, pl.ds(0, size), :] = a
    out[0, pl.ds(size, size), :] = b


def cond_product(count, *refs):
    inner, (upper, lower), outs = refs[:count], refs[count:count + 2], refs[count + 2:]
    size = inner[0].shape[1] // 2
    blk = upper.shape[2]
    both = jnp.zeros((2 * size, NX * blk), F32)
    cross = jnp.zeros((size, NX * blk), F32)
    parts = [(ref, i) for ref in inner for i in range(ref.shape[0])]
    for p, (ref, i) in enumerate(parts):
        at = pl.ds(p * NX * blk, NX * blk)
        u = jnp.concatenate([upper[i, at, :] for i in range(NX)], axis=1)
        w = jnp.concatenate([lower[i, at, :] for i in range(NX)], axis=1)
        both = both + dot(ref[i], u)
        cross = cross + dot(ref[i, pl.ds(0, size), :], w)
    result = both[:size] + both[size:] + cross
    for t in range(len(outs) // NX):

        @pl.when(pl.program_id(0) == t)
        def _():
            for i in range(NX):
                outs[t * NX + i][...] = result[:, i * blk:(i + 1) * blk]


def body(field, kf_blocks, kf_cols, kf_counts, kc_blocks, kc_cols, kc_counts):
    rows_dev, slot_count, blk, _ = kf_blocks.shape
    reach = (slot_count - 1) // 2
    size = rows_dev * blk
    edge = reach * blk
    nf, nc = lax.axis_size("form"), lax.axis_size("cond")
    nz = nc // NX
    f, c = lax.axis_index("form"), lax.axis_index("cond")
    x, z = c // nz, c % nz
    first_row = (f * nc + c) * rows_dev
    order = (4, 3, 5, 2, 6, 1, 7, 0)
    scalars = jnp.stack([first_row, f, c, c, c] + list(order)).astype(jnp.int32)

    def move(value, dx, dz):
        pairs = [
            (a * nz + b, (a ^ dx) * nz + (b + dz) % nz) for a in range(NX) for b in range(nz)
        ]
        return lax.ppermute(value, "cond", pairs)

    def gate(value, *earlier):
        return lax.optimization_barrier((value,) + earlier)[0]

    part = kc_blocks.shape[1] * blk // nf
    piece = lax.dynamic_slice_in_dim(kc_blocks.reshape(-1, blk), f * part, part, axis=0)
    total = nf * nc

    def crossed(value, flip):
        return lax.ppermute(value, ("form", "cond"), [(i, i ^ flip) for i in range(total)])

    lines = [list(range(i * nz, (i + 1) * nz)) for i in range(NX)]
    copies = jnp.broadcast_to(piece[None], (nz, part, blk))
    pieces = lax.all_to_all(copies, "cond", 0, 0, axis_index_groups=lines, tiled=True)
    field = gate(field, pieces)
    regrouped = lax.all_to_all(field.reshape(nc, size, blk), "cond", 0, 0, tiled=True)

    far, near = total // 2, nz
    pieces = jnp.stack([pieces] + [crossed(pieces, flip) for flip in (near, far, far + near)])
    pieces = pieces.reshape((NX, 1, nc, part, blk))
    pieces = jnp.concatenate([pieces] + [crossed(pieces, i * 2 * nc) for i in range(1, nf // 4)], axis=1)
    pieces = jnp.stack([pieces, crossed(pieces, nc)], axis=2).reshape((nf, nc, part, blk))

    band = rows_dev + 2 * reach
    kmid, klow, khigh = pl.pallas_call(
        form_kernel_build,
        out_shape=(
            jax.ShapeDtypeStruct((2 * size, size), BF),
            jax.ShapeDtypeStruct((2 * edge, edge), BF),
            jax.ShapeDtypeStruct((2 * edge, edge), BF),
        ),
        in_specs=[SMEM, SMEM, SMEM, pl.BlockSpec(memory_space=pltpu.VMEM)],
        scratch_shapes=[pltpu.VMEM((band, size, blk), F32)],
        compiler_params=params(8),
        cost_estimate=cost(0, 8 * MIB),
        name="form_kernel_build",
    )(scalars, kf_cols, kf_counts, kf_blocks)

    width = nc * blk
    upper, lower = pl.pallas_call(
        lambda *refs: cond_kernel_build(nz, *refs),
        grid=(nz,),
        out_shape=(pltpu.HBM((nc, width, blk), BF),) * 2,
        in_specs=[SMEM, SMEM, SMEM, pl.BlockSpec(pieces.shape, lambda t: (0, 0, 0, 0))],
        out_specs=(pl.BlockSpec((NX, width, blk), lambda t: (t, 0, 0)),) * 2,
        compiler_params=params(16),
        cost_estimate=cost(0, 32 * MIB),
        name="cond_kernel_build",
    )(scalars, kc_cols, kc_counts, pieces)

    keys = (kmid, klow, khigh, upper)
    inner = []

    def whole(a):
        return pl.BlockSpec(a.shape, lambda i: (0,) * a.ndim)

    start = 0
    for key in keys:
        per = nc // len(keys)
        columns = lax.slice_in_dim(gate(regrouped, key), start, start + per, axis=0)
        from_low = lax.ppermute(columns[:, size - edge:], ("form", "cond"), [(i, i + 1) for i in range(total - 1)])
        from_high = lax.ppermute(columns[:, :edge], ("form", "cond"), [(i + 1, i) for i in range(total - 1)])
        args = (kmid, klow, khigh)
        place = start // NX
        inner.append(pl.pallas_call(
            form_product,
            grid=(per // NX,),
            out_shape=jax.ShapeDtypeStruct((per // NX, 2 * size, NX * blk), BF),
            in_specs=[whole(a) for a in args] + [
                pl.BlockSpec((NX, size, blk), lambda i, place=place: (place + i, 0, 0)),
                pl.BlockSpec((NX, edge, blk), lambda i: (i, 0, 0)),
                pl.BlockSpec((NX, edge, blk), lambda i: (i, 0, 0)),
            ],
            out_specs=pl.BlockSpec((1, 2 * size, NX * blk), lambda i: (i, 0, 0)),
            compiler_params=params(12),
            cost_estimate=cost(0, 8 * MIB),
            name="form_product",
        )(*args, regrouped, from_low, from_high))
        start += per

    received = []
    near = [(0, 1), (0, 0), (7, 1), (1, 1), (7, 0), (1, 0)]
    calls = (
        (3, 5, near + [(6, 1), (2, 1), (6, 0), (2, 0)]),
        (1, 2, [(5, 1), (3, 1), (5, 0), (3, 0)]),
        (0, 1, [(4, 1), (4, 0)]),
    )
    for done, count, sends in calls:
        spec = pl.BlockSpec((NX, width, blk), lambda i, done=done: (done + i, 0, 0))
        results = pl.pallas_call(
            lambda *refs: cond_product(len(inner), *refs),
            grid=(count,),
            out_shape=(jax.ShapeDtypeStruct((size, blk), F32),) * (NX * count),
            in_specs=[whole(a) for a in inner] + [spec, spec],
            out_specs=(pl.BlockSpec((size, blk), lambda i: (0, 0)),) * (NX * count),
            compiler_params=params(20),
            cost_estimate=cost(0, 14 * MIB * count),
            name="cond_product",
        )(*inner, upper, lower)
        for dz, dx in sends:
            one = results[(order.index(dz) - done) * NX + dx]
            got = one if dz == 0 and dx == 0 else move(one, dx, dz)
            received.append(((x ^ dx) * nz + (z - dz) % nz, got))

    out = None
    for batch in (received[-10:], received[:-10]):
        count = len(batch)
        places = jnp.stack([place for place, _ in batch]).astype(jnp.int32)
        blocks = [block for _, block in batch] + ([] if out is None else [out])
        out = pl.pallas_call(
            lambda *refs, count=count: place_rows(count, *refs),
            out_shape=jax.ShapeDtypeStruct((nc * size, blk), F32),
            in_specs=[SMEM] + [pl.BlockSpec(memory_space=pltpu.VMEM)] * count + [pl.BlockSpec(memory_space=pltpu.HBM)] * (len(blocks) - count),
            out_specs=pl.BlockSpec(memory_space=pltpu.HBM),
            scratch_shapes=[pltpu.SemaphoreType.DMA((count,))],
            input_output_aliases={} if out is None else {len(blocks): 0},
            compiler_params=params(6),
            cost_estimate=cost(0, 4 * MIB),
            name="place_rows",
        )(places, *blocks)
    return out


def solution(mesh):
    in_specs = (
        P("form", "cond"),
        P(("form", "cond"), None, None, None),
        P(("form", "cond"), None),
        P(("form", "cond")),
        P("cond", None, None, None),
        P(),
        P(),
    )
    out_specs = P("form", "cond")
    return jax.shard_map(body, mesh=mesh, in_specs=in_specs, out_specs=out_specs, check_vma=False)
```

```python
import jax
import jax.numpy as jnp
from jax import lax
from jax.experimental import pallas as pl
from jax.experimental.pallas import tpu as pltpu
from jax.sharding import PartitionSpec as P

NX = 2
BF = jnp.bfloat16
F32 = jnp.float32
SMEM = pl.BlockSpec(memory_space=pltpu.SMEM)


MIB = 1 << 20


def params(mib):
    return pltpu.CompilerParams(vmem_limit_bytes=mib * MIB)


def cost(flops, byte):
    return pl.CostEstimate(flops=flops, transcendentals=0, bytes_accessed=byte)


def split(value):
    high = value.astype(BF)
    return high, (value - high.astype(F32)).astype(BF)


def dot(a, b):
    return jnp.dot(a, b, preferred_element_type=F32)


def form_kernel_build(scalars, cols, counts, blocks, mid, low, high, dense):
    rows, slots, blk, _ = blocks.shape
    reach = (slots - 1) // 2
    dense[...] = jnp.zeros_like(dense)
    for k in range(rows):
        for s in range(slots):
            place = cols[k, s] - scalars[0] + reach

            @pl.when(s < counts[k])
            def _():
                dense[place, pl.ds(k * blk, blk), :] = blocks[k, s]

    size = rows * blk
    half = reach * blk
    for j in range(rows):
        a, b = split(dense[reach + j])
        mid[pl.ds(0, size), pl.ds(j * blk, blk)] = a
        mid[pl.ds(size, size), pl.ds(j * blk, blk)] = b
    for j in range(reach):
        a, b = split(dense[j, pl.ds(0, half), :])
        low[pl.ds(0, half), pl.ds(j * blk, blk)] = a
        low[pl.ds(half, half), pl.ds(j * blk, blk)] = b
        a, b = split(dense[reach + rows + j, pl.ds(size - half, half), :])
        high[pl.ds(0, half), pl.ds(j * blk, blk)] = a
        high[pl.ds(half, half), pl.ds(j * blk, blk)] = b


def cond_kernel_build(nz, scalars, cols, counts, pieces, upper, lower):
    nf, nb, part, blk = pieces.shape
    slots = cols.shape[1]
    per = blk // part
    step = pl.program_id(0)
    f, c = scalars[1], scalars[2]
    bits = nz.bit_length() - 1
    x, wanted = c >> bits, (c + scalars[5 + step]) & (nz - 1)
    upper[...] = jnp.zeros_like(upper)
    lower[...] = jnp.zeros_like(lower)

    def source(q, carry):
        for slot in range(slots):
            d = cols[q, slot]
            tdx = (d >> bits) ^ x

            @pl.when((slot < counts[q]) & ((d & (nz - 1)) == wanted))
            def _():
                for i in range(per):
                    a, b = split(pieces[f ^ (slot * per + i), q ^ (x << bits)])
                    at = pl.ds(pl.multiple_of(q * blk + i * part, part), part)
                    upper[tdx, at, :] = a
                    lower[tdx, at, :] = b

        return carry

    lax.fori_loop(0, nb, source, 0)


def place_rows(count, scalars, *refs):
    blocks, out, sems = refs[:count], refs[-2], refs[-1]
    size = blocks[0].shape[0]
    copies = [
        pltpu.make_async_copy(block, out.at[pl.ds(scalars[i] * size, size), :], sems.at[i])
        for i, block in enumerate(blocks)
    ]
    for copy in copies:
        copy.start()
    for copy in copies:
        copy.wait()


def form_product(kmid, klow, khigh, field, low, high, out):
    def beside(ref):
        return jnp.concatenate([ref[i] for i in range(NX)], axis=1)

    size = field.shape[1]
    half = low.shape[1]

    def three(k, v):
        n = k.shape[0] // 2
        a, b = split(v)
        both = dot(k[...], a)
        return both[:n] + both[n:] + dot(k[pl.ds(0, n), :], b)

    total = three(kmid, beside(field))
    top = total[:half] + three(klow, beside(low))
    bottom = total[size - half:] + three(khigh, beside(high))
    inside = [total[half:size - half]] if size > 2 * half else []
    a, b = split(jnp.concatenate([top] + inside + [bottom], axis=0))
    out[0, pl.ds(0, size), :] = a
    out[0, pl.ds(size, size), :] = b


def cond_product(count, first, carried, *refs):
    inner, (upper, lower), outs = refs[:count], refs[count:count + 2], refs[count + 2 + carried:]
    size = inner[0].shape[1] // 2
    blk = upper.shape[2]
    both = jnp.zeros((2 * size, NX * blk), F32)
    cross = jnp.zeros((size, NX * blk), F32)
    parts = [(ref, i) for ref in inner for i in range(ref.shape[0])]
    for p, (ref, i) in enumerate(parts, first):
        at = pl.ds(p * NX * blk, NX * blk)
        u = jnp.concatenate([upper[i, at, :] for i in range(NX)], axis=1)
        w = jnp.concatenate([lower[i, at, :] for i in range(NX)], axis=1)
        both = both + dot(ref[i], u)
        cross = cross + dot(ref[i, pl.ds(0, size), :], w)
    result = both[:size] + both[size:] + cross
    if carried:
        result = result + refs[count + 2][...]
    if len(outs) == 1:
        outs[0][...] = result
        return
    for t in range(len(outs) // NX):

        @pl.when(pl.program_id(0) == t)
        def _():
            for i in range(NX):
                outs[t * NX + i][...] = result[:, i * blk:(i + 1) * blk]


def body(field, kf_blocks, kf_cols, kf_counts, kc_blocks, kc_cols, kc_counts):
    rows_dev, slot_count, blk, _ = kf_blocks.shape
    reach = (slot_count - 1) // 2
    size = rows_dev * blk
    edge = reach * blk
    nf, nc = lax.axis_size("form"), lax.axis_size("cond")
    nz = nc // NX
    f, c = lax.axis_index("form"), lax.axis_index("cond")
    x, z = c // nz, c % nz
    first_row = (f * nc + c) * rows_dev
    order = (4, 3, 5, 2, 6, 1, 7, 0)
    scalars = jnp.stack([first_row, f, c, c, c] + list(order)).astype(jnp.int32)

    def move(value, dx, dz):
        pairs = [
            (a * nz + b, (a ^ dx) * nz + (b + dz) % nz) for a in range(NX) for b in range(nz)
        ]
        return lax.ppermute(value, "cond", pairs)

    def gate(value, *earlier):
        return lax.optimization_barrier((value,) + earlier)[0]

    part = kc_blocks.shape[1] * blk // nf
    piece = lax.dynamic_slice_in_dim(kc_blocks.reshape(-1, blk), f * part, part, axis=0)
    total = nf * nc

    def crossed(value, flip):
        return lax.ppermute(value, ("form", "cond"), [(i, i ^ flip) for i in range(total)])

    lines = [list(range(i * nz, (i + 1) * nz)) for i in range(NX)]
    copies = jnp.broadcast_to(piece[None], (nz, part, blk))
    pieces = lax.all_to_all(copies, "cond", 0, 0, axis_index_groups=lines, tiled=True)
    field = gate(field, pieces)
    regrouped = lax.all_to_all(field.reshape(nc, size, blk), "cond", 0, 0, tiled=True)

    far, near = total // 2, nz
    pieces = jnp.stack([pieces] + [crossed(pieces, flip) for flip in (near, far, far + near)])
    pieces = pieces.reshape((NX, 1, nc, part, blk))
    pieces = jnp.concatenate([pieces] + [crossed(pieces, i * 2 * nc) for i in range(1, nf // 4)], axis=1)
    pieces = jnp.stack([pieces, crossed(pieces, nc)], axis=2).reshape((nf, nc, part, blk))

    band = rows_dev + 2 * reach
    kmid, klow, khigh = pl.pallas_call(
        form_kernel_build,
        out_shape=(
            jax.ShapeDtypeStruct((2 * size, size), BF),
            jax.ShapeDtypeStruct((2 * edge, edge), BF),
            jax.ShapeDtypeStruct((2 * edge, edge), BF),
        ),
        in_specs=[SMEM, SMEM, SMEM, pl.BlockSpec(memory_space=pltpu.VMEM)],
        scratch_shapes=[pltpu.VMEM((band, size, blk), F32)],
        compiler_params=params(8),
        cost_estimate=cost(0, 8 * MIB),
        name="form_kernel_build",
    )(scalars, kf_cols, kf_counts, kf_blocks)

    width = nc * blk
    upper, lower = pl.pallas_call(
        lambda *refs: cond_kernel_build(nz, *refs),
        grid=(nz,),
        out_shape=(pltpu.HBM((nc, width, blk), BF),) * 2,
        in_specs=[SMEM, SMEM, SMEM, pl.BlockSpec(pieces.shape, lambda t: (0, 0, 0, 0))],
        out_specs=(pl.BlockSpec((NX, width, blk), lambda t: (t, 0, 0)),) * 2,
        compiler_params=params(16),
        cost_estimate=cost(0, 32 * MIB),
        name="cond_kernel_build",
    )(scalars, kc_cols, kc_counts, pieces)

    keys = (kmid, klow, khigh)
    inner = []

    def whole(a):
        return pl.BlockSpec(a.shape, lambda i: (0,) * a.ndim)

    start = 0
    for key, per in zip(keys, (8, 6, 2)):
        columns = lax.slice_in_dim(gate(regrouped, key, upper), start, start + per, axis=0)
        from_low = lax.ppermute(columns[:, size - edge:], ("form", "cond"), [(i, i + 1) for i in range(total - 1)])
        from_high = lax.ppermute(columns[:, :edge], ("form", "cond"), [(i + 1, i) for i in range(total - 1)])
        args = (kmid if not inner else gate(kmid, inner[-1]), klow, khigh)
        place = start // NX
        inner.append(pl.pallas_call(
            form_product,
            grid=(per // NX,),
            out_shape=jax.ShapeDtypeStruct((per // NX, 2 * size, NX * blk), BF),
            in_specs=[whole(a) for a in args] + [
                pl.BlockSpec((NX, size, blk), lambda i, place=place: (place + i, 0, 0)),
                pl.BlockSpec((NX, edge, blk), lambda i: (i, 0, 0)),
                pl.BlockSpec((NX, edge, blk), lambda i: (i, 0, 0)),
            ],
            out_specs=pl.BlockSpec((1, 2 * size, NX * blk), lambda i: (i, 0, 0)),
            compiler_params=params(12),
            cost_estimate=cost(0, 8 * MIB),
            name="form_product",
        )(*args, regrouped, from_low, from_high))
        start += per

    received = []
    near = [(0, 1), (0, 0), (7, 1), (1, 1), (7, 0), (1, 0)]
    calls = (
        (3, 5, near + [(6, 1), (2, 1), (6, 0), (2, 0)]),
        (1, 2, [(5, 1), (3, 1), (5, 0), (3, 0)]),
        (0, 1, [(4, 1), (4, 0)]),
    )
    def product(blocks, first, carry, done, count, outs):
        spec = pl.BlockSpec((NX, width, blk), lambda i: (done + i, 0, 0))
        return pl.pallas_call(
            lambda *refs: cond_product(len(blocks), first, len(carry), *refs),
            grid=(count,),
            out_shape=outs,
            in_specs=[whole(a) for a in blocks] + [spec, spec] + [whole(a) for a in carry],
            out_specs=tuple(pl.BlockSpec(o.shape, lambda i: (0, 0)) for o in outs),
            compiler_params=params(20),
            cost_estimate=cost(0, 14 * MIB * count),
            name="cond_product",
        )(*blocks, upper, lower, *carry)

    known = sum(a.shape[0] for a in inner[:-1])
    early = product(inner[:-1], 0, (), 0, 1, (jax.ShapeDtypeStruct((size, NX * blk), F32),))
    for done, count, sends in calls:
        outs = (jax.ShapeDtypeStruct((size, blk), F32),) * (NX * count)
        if done:
            results = product(inner, 0, (), done, count, outs)
        else:
            results = product(inner[-1:], known, tuple(early), done, count, outs)
        for dz, dx in sends:
            one = results[(order.index(dz) - done) * NX + dx]
            got = one if dz == 0 and dx == 0 else move(one, dx, dz)
            received.append(((x ^ dx) * nz + (z - dz) % nz, got))

    out = None
    for batch in (received[-10:], received[:-10]):
        count = len(batch)
        places = jnp.stack([place for place, _ in batch]).astype(jnp.int32)
        blocks = [block for _, block in batch] + ([] if out is None else [out])
        out = pl.pallas_call(
            lambda *refs, count=count: place_rows(count, *refs),
            out_shape=jax.ShapeDtypeStruct((nc * size, blk), F32),
            in_specs=[SMEM] + [pl.BlockSpec(memory_space=pltpu.VMEM)] * count + [pl.BlockSpec(memory_space=pltpu.HBM)] * (len(blocks) - count),
            out_specs=pl.BlockSpec(memory_space=pltpu.HBM),
            scratch_shapes=[pltpu.SemaphoreType.DMA((count,))],
            input_output_aliases={} if out is None else {len(blocks): 0},
            compiler_params=params(6),
            cost_estimate=cost(0, 4 * MIB),
            name="place_rows",
        )(places, *blocks)
    return out


def solution(mesh):
    in_specs = (
        P("form", "cond"),
        P(("form", "cond"), None, None, None),
        P(("form", "cond"), None),
        P(("form", "cond")),
        P("cond", None, None, None),
        P(),
        P(),
    )
    out_specs = P("form", "cond")
    return jax.shard_map(body, mesh=mesh, in_specs=in_specs, out_specs=out_specs, check_vma=False)
```

```python
import jax
import jax.numpy as jnp
from jax import lax
from jax.experimental import pallas as pl
from jax.experimental.pallas import tpu as pltpu
from jax.sharding import PartitionSpec as P

NX = 2
BF = jnp.bfloat16
F32 = jnp.float32
SMEM = pl.BlockSpec(memory_space=pltpu.SMEM)


MIB = 1 << 20


def params(mib):
    return pltpu.CompilerParams(vmem_limit_bytes=mib * MIB)


def cost(flops, byte):
    return pl.CostEstimate(flops=flops, transcendentals=0, bytes_accessed=byte)


def split(value):
    high = value.astype(BF)
    return high, (value - high.astype(F32)).astype(BF)


def dot(a, b):
    return jnp.dot(a, b, preferred_element_type=F32)


def form_kernel_build(scalars, cols, counts, blocks, mid, low, high, dense):
    rows, slots, blk, _ = blocks.shape
    reach = (slots - 1) // 2
    dense[...] = jnp.zeros_like(dense)
    for k in range(rows):
        for s in range(slots):
            place = cols[k, s] - scalars[0] + reach

            @pl.when(s < counts[k])
            def _():
                dense[place, pl.ds(k * blk, blk), :] = blocks[k, s]

    size = rows * blk
    half = reach * blk
    for j in range(rows):
        a, b = split(dense[reach + j])
        mid[pl.ds(0, size), pl.ds(j * blk, blk)] = a
        mid[pl.ds(size, size), pl.ds(j * blk, blk)] = b
    for j in range(reach):
        a, b = split(dense[j, pl.ds(0, half), :])
        low[pl.ds(0, half), pl.ds(j * blk, blk)] = a
        low[pl.ds(half, half), pl.ds(j * blk, blk)] = b
        a, b = split(dense[reach + rows + j, pl.ds(size - half, half), :])
        high[pl.ds(0, half), pl.ds(j * blk, blk)] = a
        high[pl.ds(half, half), pl.ds(j * blk, blk)] = b


def cond_kernel_build(nz, scalars, cols, counts, pieces, upper, lower):
    nf, nb, part, blk = pieces.shape
    slots = cols.shape[1]
    per = blk // part
    step = pl.program_id(0)
    f, c = scalars[1], scalars[2]
    bits = nz.bit_length() - 1
    x, wanted = c >> bits, (c + scalars[5 + step]) & (nz - 1)
    upper[...] = jnp.zeros_like(upper)
    lower[...] = jnp.zeros_like(lower)

    def source(q, carry):
        for slot in range(slots):
            d = cols[q, slot]
            tdx = (d >> bits) ^ x

            @pl.when((slot < counts[q]) & ((d & (nz - 1)) == wanted))
            def _():
                for i in range(per):
                    a, b = split(pieces[f ^ (slot * per + i), q ^ (x << bits)])
                    at = pl.ds(pl.multiple_of(q * blk + i * part, part), part)
                    upper[tdx, at, :] = a
                    lower[tdx, at, :] = b

        return carry

    lax.fori_loop(0, nb, source, 0)


def place_rows(count, scalars, *refs):
    blocks, out, sems = refs[:count], refs[-2], refs[-1]
    size = blocks[0].shape[0]
    copies = [
        pltpu.make_async_copy(block, out.at[pl.ds(scalars[i] * size, size), :], sems.at[i])
        for i, block in enumerate(blocks)
    ]
    for copy in copies:
        copy.start()
    for copy in copies:
        copy.wait()


def form_product(kmid, klow, khigh, field, low, high, out):
    def beside(ref):
        return jnp.concatenate([ref[i] for i in range(NX)], axis=1)

    size = field.shape[1]
    half = low.shape[1]

    def three(k, v):
        n = k.shape[0] // 2
        a, b = split(v)
        both = dot(k[...], a)
        return both[:n] + both[n:] + dot(k[pl.ds(0, n), :], b)

    total = three(kmid, beside(field))
    top = total[:half] + three(klow, beside(low))
    bottom = total[size - half:] + three(khigh, beside(high))
    inside = [total[half:size - half]] if size > 2 * half else []
    a, b = split(jnp.concatenate([top] + inside + [bottom], axis=0))
    out[0, pl.ds(0, size), :] = a
    out[0, pl.ds(size, size), :] = b


def cond_product(count, first, carried, *refs):
    inner, (upper, lower), outs = refs[:count], refs[count:count + 2], refs[count + 2 + carried:]
    size = inner[0].shape[1] // 2
    blk = upper.shape[2]
    both = jnp.zeros((2 * size, NX * blk), F32)
    cross = jnp.zeros((size, NX * blk), F32)
    parts = [(ref, i) for ref in inner for i in range(ref.shape[0])]
    for p, (ref, i) in enumerate(parts, first):
        at = pl.ds(p * NX * blk, NX * blk)
        u = jnp.concatenate([upper[i, at, :] for i in range(NX)], axis=1)
        w = jnp.concatenate([lower[i, at, :] for i in range(NX)], axis=1)
        both = both + dot(ref[i], u)
        cross = cross + dot(ref[i, pl.ds(0, size), :], w)
    result = both[:size] + both[size:] + cross
    if carried:
        result = result + refs[count + 2][...]
    if len(outs) == 1:
        outs[0][...] = result
        return
    for t in range(len(outs) // NX):

        @pl.when(pl.program_id(0) == t)
        def _():
            for i in range(NX):
                outs[t * NX + i][...] = result[:, i * blk:(i + 1) * blk]


def body(field, kf_blocks, kf_cols, kf_counts, kc_blocks, kc_cols, kc_counts):
    rows_dev, slot_count, blk, _ = kf_blocks.shape
    reach = (slot_count - 1) // 2
    size = rows_dev * blk
    edge = reach * blk
    nf, nc = lax.axis_size("form"), lax.axis_size("cond")
    nz = nc // NX
    f, c = lax.axis_index("form"), lax.axis_index("cond")
    x, z = c // nz, c % nz
    first_row = (f * nc + c) * rows_dev
    order = (4, 3, 5, 2, 6, 1, 7, 0)
    scalars = jnp.stack([first_row, f, c, c, c] + list(order)).astype(jnp.int32)

    def move(value, dx, dz):
        pairs = [
            (a * nz + b, (a ^ dx) * nz + (b + dz) % nz) for a in range(NX) for b in range(nz)
        ]
        return lax.ppermute(value, "cond", pairs)

    def gate(value, *earlier):
        return lax.optimization_barrier((value,) + earlier)[0]

    part = kc_blocks.shape[1] * blk // nf
    piece = lax.dynamic_slice_in_dim(kc_blocks.reshape(-1, blk), f * part, part, axis=0)
    total = nf * nc

    def crossed(value, flip):
        return lax.ppermute(value, ("form", "cond"), [(i, i ^ flip) for i in range(total)])

    lines = [list(range(i * nz, (i + 1) * nz)) for i in range(NX)]
    copies = jnp.broadcast_to(piece[None], (nz, part, blk))
    pieces = lax.all_to_all(copies, "cond", 0, 0, axis_index_groups=lines, tiled=True)
    field = gate(field, pieces)
    regrouped = lax.all_to_all(field.reshape(nc, size, blk), "cond", 0, 0, tiled=True)

    far, near = total // 2, nz
    pieces = jnp.stack([pieces] + [crossed(pieces, flip) for flip in (near, far, far + near)])
    pieces = pieces.reshape((NX, 1, nc, part, blk))
    pieces = jnp.concatenate([pieces] + [crossed(pieces, i * 2 * nc) for i in range(1, nf // 4)], axis=1)
    pieces = jnp.stack([pieces, crossed(pieces, nc)], axis=2).reshape((nf, nc, part, blk))

    band = rows_dev + 2 * reach
    kmid, klow, khigh = pl.pallas_call(
        form_kernel_build,
        out_shape=(
            jax.ShapeDtypeStruct((2 * size, size), BF),
            jax.ShapeDtypeStruct((2 * edge, edge), BF),
            jax.ShapeDtypeStruct((2 * edge, edge), BF),
        ),
        in_specs=[SMEM, SMEM, SMEM, pl.BlockSpec(memory_space=pltpu.VMEM)],
        scratch_shapes=[pltpu.VMEM((band, size, blk), F32)],
        compiler_params=params(8),
        cost_estimate=cost(0, 8 * MIB),
        name="form_kernel_build",
    )(scalars, kf_cols, kf_counts, kf_blocks)

    width = nc * blk
    upper, lower = pl.pallas_call(
        lambda *refs: cond_kernel_build(nz, *refs),
        grid=(nz,),
        out_shape=(pltpu.HBM((nc, width, blk), BF),) * 2,
        in_specs=[SMEM, SMEM, SMEM, pl.BlockSpec(pieces.shape, lambda t: (0, 0, 0, 0))],
        out_specs=(pl.BlockSpec((NX, width, blk), lambda t: (t, 0, 0)),) * 2,
        compiler_params=params(16),
        cost_estimate=cost(0, 32 * MIB),
        name="cond_kernel_build",
    )(scalars, kc_cols, kc_counts, pieces)

    keys = (kmid, klow, khigh)
    inner = []

    def whole(a):
        return pl.BlockSpec(a.shape, lambda i: (0,) * a.ndim)

    start = 0
    for key, per in zip(keys, (8, 6, 2)):
        columns = lax.slice_in_dim(gate(regrouped, key, upper), start, start + per, axis=0)
        from_low = lax.ppermute(columns[:, size - edge:], ("form", "cond"), [(i, i + 1) for i in range(total - 1)])
        from_high = lax.ppermute(columns[:, :edge], ("form", "cond"), [(i + 1, i) for i in range(total - 1)])
        args = (kmid if not inner else gate(kmid, inner[-1]), klow, khigh)
        place = start // NX
        inner.append(pl.pallas_call(
            form_product,
            grid=(per // NX,),
            out_shape=jax.ShapeDtypeStruct((per // NX, 2 * size, NX * blk), BF),
            in_specs=[whole(a) for a in args] + [
                pl.BlockSpec((NX, size, blk), lambda i, place=place: (place + i, 0, 0)),
                pl.BlockSpec((NX, edge, blk), lambda i: (i, 0, 0)),
                pl.BlockSpec((NX, edge, blk), lambda i: (i, 0, 0)),
            ],
            out_specs=pl.BlockSpec((1, 2 * size, NX * blk), lambda i: (i, 0, 0)),
            compiler_params=params(12),
            cost_estimate=cost(0, 8 * MIB),
            name="form_product",
        )(*args, regrouped, from_low, from_high))
        start += per

    received = []
    near = [(0, 1), (0, 0), (7, 1), (1, 1), (7, 0), (1, 0)]
    calls = (
        (5, 3, near),
        (3, 2, [(6, 1), (2, 1), (6, 0), (2, 0)]),
        (1, 2, [(5, 1), (3, 1), (5, 0), (3, 0)]),
        (0, 1, [(4, 1), (4, 0)]),
    )
    def product(blocks, first, carry, done, count, outs):
        spec = pl.BlockSpec((NX, width, blk), lambda i: (done + i, 0, 0))
        return pl.pallas_call(
            lambda *refs: cond_product(len(blocks), first, len(carry), *refs),
            grid=(count,),
            out_shape=outs,
            in_specs=[whole(a) for a in blocks] + [spec, spec] + [whole(a) for a in carry],
            out_specs=tuple(pl.BlockSpec(o.shape, lambda i: (0, 0)) for o in outs),
            compiler_params=params(20),
            cost_estimate=cost(0, 14 * MIB * count),
            name="cond_product",
        )(*blocks, upper, lower, *carry)

    known = sum(a.shape[0] for a in inner[:-1])
    early = product(inner[:-1], 0, (), 0, 1, (jax.ShapeDtypeStruct((size, NX * blk), F32),))
    for done, count, sends in calls:
        outs = (jax.ShapeDtypeStruct((size, blk), F32),) * (NX * count)
        if done:
            results = product(inner, 0, (), done, count, outs)
        else:
            results = product(inner[-1:], known, tuple(early), done, count, outs)
        for dz, dx in sends:
            one = results[(order.index(dz) - done) * NX + dx]
            got = one if dz == 0 and dx == 0 else move(one, dx, dz)
            received.append(((x ^ dx) * nz + (z - dz) % nz, got))

    out = None
    for batch in (received[-10:], received[:-10]):
        count = len(batch)
        places = jnp.stack([place for place, _ in batch]).astype(jnp.int32)
        blocks = [block for _, block in batch] + ([] if out is None else [out])
        out = pl.pallas_call(
            lambda *refs, count=count: place_rows(count, *refs),
            out_shape=jax.ShapeDtypeStruct((nc * size, blk), F32),
            in_specs=[SMEM] + [pl.BlockSpec(memory_space=pltpu.VMEM)] * count + [pl.BlockSpec(memory_space=pltpu.HBM)] * (len(blocks) - count),
            out_specs=pl.BlockSpec(memory_space=pltpu.HBM),
            scratch_shapes=[pltpu.SemaphoreType.DMA((count,))],
            input_output_aliases={} if out is None else {len(blocks): 0},
            compiler_params=params(6),
            cost_estimate=cost(0, 4 * MIB),
            name="place_rows",
        )(places, *blocks)
    return out


def solution(mesh):
    in_specs = (
        P("form", "cond"),
        P(("form", "cond"), None, None, None),
        P(("form", "cond"), None),
        P(("form", "cond")),
        P("cond", None, None, None),
        P(),
        P(),
    )
    out_specs = P("form", "cond")
    return jax.shard_map(body, mesh=mesh, in_specs=in_specs, out_specs=out_specs, check_vma=False)
```
